32 devices in a mesh: row: 8 (over z, x), col: 4 (over y, core).
Axes of the slice: x: 2, y: 2, z: 4, core: 2. Of those that a mesh axis runs over, the one named last changes fastest.
Arguments:
- vertex: bfloat16 [64, 4096, 4096], P(None, 'row', 'col'), may hold values from -6 to 6
- a_factor: bfloat16 [4096, 1024], P('row', 'col'), as said below
- b_factor: bfloat16 [4096, 1024], P('col', 'row'), as said below
Outputs:
- field_factor: float32 [64, 1024], P(None, 'col')
The draws below stay inside these ranges and needn't reach their ends.
Inputs may be any that keep to these rules, and one draw needn't show every extreme that they name: `a_factor`: entries lie within -12 / sqrt(4096) and 12 / sqrt(4096). `b_factor`: entries lie within -12 / sqrt(4096) and 12 / sqrt(4096).
All inputs are finite; a program needn't handle non-finite values.
Results may differ from the reference program's by a relative error of at most 0.0003.
Values may be sent and summed in bfloat16 or wider, within the bound.
No kernel may reach another device: no remote copies, remote signals or barrier semaphores. Data moves between devices by JAX's collectives and lax.ppermute only.
A program may use at most 128 MiB of HBM per device.

```python
import jax
import jax.numpy as jnp
from jax import lax

NP = 4096
NQ = 4096
R = 1024
NG = 64


def factor_draw(key, count):
    first = jax.random.fold_in(key, 0)
    second = jax.random.fold_in(key, 1)
    fourth = jax.random.fold_in(key, 3)
    latent = jnp.clip(jax.random.normal(second, (count, 8), jnp.float32), -4.0, 4.0)
    levels = jnp.exp(jnp.linspace(jnp.log(0.1), jnp.log(3.0), 8).astype(jnp.float32))
    mixing = jnp.clip(jax.random.normal(fourth, (8, R), jnp.float32), -4.0, 4.0) * (0.25 * jnp.sqrt(levels))[:, None]
    shared = jnp.sum(latent[:, :, None] * mixing[None, :, :], axis=1)
    noise = jnp.clip(jax.random.normal(first, (count, R), jnp.float32), -4.0, 4.0)
    raw = jnp.clip(0.5 * noise + shared, -11.9, 11.9)
    values = raw / jnp.sqrt(jnp.float32(count))
    return values.astype(jnp.bfloat16)


def draw_a_factor(key, part):
    return factor_draw(jax.random.fold_in(key, 11), NP)


def draw_b_factor(key, part):
    return factor_draw(jax.random.fold_in(key, 23), NQ)


def block_scale(rng, dims, shards, low, top_value):
    def one(position, parts):
        steps = jax.random.uniform(jax.random.fold_in(jax.random.fold_in(rng, 6), position), (parts,), jnp.float32, low / len(shards), top_value / len(shards))
        return jnp.repeat(jnp.exp(steps), dims[position] // parts).reshape((-1,) + (1,) * (len(dims) - position - 1))

    gain = one(*shards[0])
    for cut in shards[1:]:
        gain = gain * one(*cut)
    return gain


def centred(rng, shape, width, most, cuts=(), held_as=jnp.bfloat16):
    drawn = width * jax.random.normal(rng, shape, jnp.float32)
    if cuts:
        drawn = drawn * block_scale(rng, shape, cuts, -0.22, 0.18)
    return jnp.clip(drawn, -most, most).astype(held_as)


def setup_inputs(seed: int = 0) -> dict:
    streams_of = jax.random.split(jax.random.key(seed), 4)
    vertex = centred(streams_of[0], (NG, NP, NQ), 1.0, 6.0, ((1, 8), (2, 4)))
    a_factor = draw_a_factor(jax.random.fold_in(streams_of[3], 71), 0)
    b_factor = draw_b_factor(jax.random.fold_in(streams_of[3], 71), 0)
    return dict(vertex=vertex, a_factor=a_factor, b_factor=b_factor)


ridge_term = 0.25

def reference(vertex, a_factor, b_factor):
    a_wide = a_factor.astype(jnp.float32)
    b_wide = b_factor.astype(jnp.float32)

    def one_field(slab):
        product = jnp.dot(slab.astype(jnp.float32), b_wide, precision=lax.Precision.HIGHEST)
        return jnp.sum(product * a_wide, axis=0)
    m_total = lax.map(one_field, vertex)
    gram_a = jnp.dot(a_factor.T.astype(jnp.float32), a_factor.astype(jnp.float32), preferred_element_type=jnp.float32)
    gram_b = jnp.dot(b_factor.T.astype(jnp.float32), b_factor.astype(jnp.float32), preferred_element_type=jnp.float32)
    weight = gram_a * gram_b + ridge_term * jnp.eye(R, dtype=jnp.float32)
    factor_lower = jnp.linalg.cholesky(weight)
    solved = jax.scipy.linalg.cho_solve((factor_lower, True), m_total.T)
    return solved.T
```

```python
import functools

import jax
import jax.numpy as jnp
from jax import lax
from jax.experimental import pallas as pl
from jax.experimental.pallas import tpu as pltpu
from jax.sharding import PartitionSpec as P

ridge_term = 0.25
NB = 128
HIGHEST = lax.Precision.HIGHEST
MIB = 1 << 20


def dot_nt(x, y):
    return lax.dot_general(
        x, y, (((1,), (1,)), ((), ())), precision=HIGHEST, preferred_element_type=jnp.float32
    )


def dot_nn(x, y):
    return lax.dot_general(
        x, y, (((1,), (0,)), ((), ())), precision=HIGHEST, preferred_element_type=jnp.float32
    )


def dot_tn(x, y):
    return lax.dot_general(x, y, (((0,), (0,)), ((), ())), preferred_element_type=jnp.float32)


def row_of(v, j):
    return jnp.broadcast_to(v[j : j + 1, :], v.shape)


def col_of(v, j):
    return jnp.broadcast_to(v[:, j : j + 1], v.shape)


def invert_factor(rows):
    count = len(rows)
    lane = lax.broadcasted_iota(jnp.int32, (8, NB), 1)
    sub = lax.broadcasted_iota(jnp.int32, (8, NB), 0)
    rows = list(rows)
    scale = [None] * count
    for g in range(count):
        base = 8 * g
        cur = rows[g]
        cols = [col_of(cur, base + j) for j in range(8)]
        below = [[col_of(rows[i], base + j) for j in range(8)] for i in range(g + 1, count)]
        own = (lane >= base) & (lane < base + 8)
        cur = jnp.where(own, jnp.where(lane == sub + base, 1.0, 0.0), cur)
        forward = cur
        inverse = None
        for j in range(8):
            inv = 1.0 / row_of(cols[j], j)
            here = sub == j
            pivot = row_of(cur, j)
            forward = jnp.where(here, cur, forward)
            inverse = inv if inverse is None else jnp.where(here, inv, inverse)
            mult = cols[j] * inv
            for k in range(j + 1, 8):
                ck = row_of(cols[k], j)
                cols[k] = jnp.where(here, ck * inv, cols[k] - mult * ck)
            cur = jnp.where(here, pivot * inv, cur - mult * pivot)
        picks = [row_of(cur, j) for j in range(8)]
        for t, i in enumerate(range(g + 1, count)):
            prods = [below[t][j] * picks[j] for j in range(8)]
            while len(prods) > 1:
                prods = [prods[s] + prods[s + 1] for s in range(0, len(prods), 2)]
            rows[i] = jnp.where(own, 0.0, rows[i]) - prods[0]
        rows[g] = forward
        scale[g] = jnp.sqrt(inverse)
    return [jnp.where(lane <= sub + 8 * g, rows[g], 0.0) * scale[g] for g in range(count)]


def blk(i):
    return pl.ds(pl.multiple_of(i * NB, NB), NB)


def factor_and_solve(work, z, linv):
    nk = work.shape[0]

    def step(k, _):
        rows = [work[k, pl.ds(pl.multiple_of(k * NB + 8 * g, 8), 8), :] for g in range(NB // 8)]
        for g, v in enumerate(invert_factor(rows)):
            linv[k, 8 * g : 8 * g + 8, :] = v
        inverse = linv[k]
        z[:, blk(k)] = dot_nt(z[:, blk(k)], inverse)

        def panel(i, _):
            work[k, blk(i), :] = dot_nt(work[k, blk(i), :], inverse)
            return 0

        lax.fori_loop(k + 1, nk, panel, 0)

        def column(j, _):
            pj = work[k, blk(j), :]
            z[:, blk(j)] -= dot_nt(z[:, blk(k)], pj)

            def tile(i, _):
                work[j, blk(i), :] -= dot_nt(work[k, blk(i), :], pj)
                return 0

            lax.fori_loop(j, nk, tile, 0)
            return 0

        lax.fori_loop(k + 1, nk, column, 0)
        return 0

    lax.fori_loop(0, nk, step, 0)

    def back(t, _):
        k = nk - 1 - t
        xk = dot_nn(z[:, blk(k)], linv[k])
        z[:, blk(k)] = xk

        def update(i, _):
            z[:, blk(i)] -= dot_nn(xk, work[i, blk(k), :])
            return 0

        lax.fori_loop(0, k, update, 0)
        return 0

    lax.fori_loop(0, nk, back, 0)


def solve_kernel(tiles, pos, *refs):
    pieces, (m_ref, x_ref, work, z, linv, sem) = refs[: len(tiles)], refs[len(tiles) :]
    copies = []
    for piece, offsets in zip(pieces, tiles):
        for t, (row_off, col_off) in enumerate(offsets):
            height = piece.shape[1]
            at = pl.multiple_of((pos[1] ^ col_off) * height, height)
            target = work.at[pos[0] ^ row_off, pl.ds(at, height), :]
            copies.append(pltpu.make_async_copy(piece.at[t], target, sem.at[len(copies)]))
            copies[-1].start()
    z[...] = m_ref[...]
    for copy in copies:
        copy.wait()
    factor_and_solve(work, z, linv)
    x_ref[...] = z[...]


def solve(pos, pieces, tiles, m_total):
    rank = m_total.shape[1]
    total = sum(len(t) for t in tiles)
    return pl.pallas_call(
        functools.partial(solve_kernel, tiles),
        out_shape=jax.ShapeDtypeStruct(m_total.shape, jnp.float32),
        in_specs=[pl.BlockSpec(memory_space=pltpu.SMEM)]
        + [pl.BlockSpec(memory_space=pl.ANY)] * len(pieces)
        + [pl.BlockSpec(memory_space=pltpu.VMEM)],
        out_specs=pl.BlockSpec(memory_space=pltpu.VMEM),
        scratch_shapes=[
            pltpu.VMEM((rank // NB, rank, NB), jnp.float32),
            pltpu.VMEM(m_total.shape, jnp.float32),
            pltpu.VMEM((rank // NB, NB, NB), jnp.float32),
            pltpu.SemaphoreType.DMA((total,)),
        ],
        compiler_params=pltpu.CompilerParams(vmem_limit_bytes=24 * MIB),
        cost_estimate=pl.CostEstimate(flops=40_000_000_000, bytes_accessed=4 * rank * rank, transcendentals=0),
    )(pos, *pieces, m_total)


def contract_kernel(index, v_ref, b_ref, a_ref, o_ref):
    fields, p_local, q_local = v_ref.shape
    for n in range(b_ref.shape[0]):
        width = b_ref.shape[2]
        at = pl.multiple_of(index[n] * width, width)
        a_cols = a_ref[:, pl.ds(at, width)]
        for f in range(fields):
            product = jnp.dot(v_ref[f], b_ref[n], preferred_element_type=jnp.float32)
            o_ref[0, f : f + 1, n * width : (n + 1) * width] = jnp.sum(product * a_cols, axis=0, keepdims=True)


def contract(index, vertex, b_blocks, a_wide):
    fields, p_local, q_local = vertex.shape
    count, _, width = b_blocks.shape
    step = 4
    out = pl.pallas_call(
        contract_kernel,
        out_shape=jax.ShapeDtypeStruct((fields // step, step, count * width), jnp.float32),
        grid_spec=pltpu.PrefetchScalarGridSpec(
            num_scalar_prefetch=1,
            grid=(fields // step,),
            in_specs=[
                pl.BlockSpec((step, p_local, q_local), lambda i, s: (i, 0, 0)),
                pl.BlockSpec(b_blocks.shape, lambda i, s: (0, 0, 0)),
                pl.BlockSpec(a_wide.shape, lambda i, s: (0, 0)),
            ],
            out_specs=pl.BlockSpec((1, step, count * width), lambda i, s: (i, 0, 0)),
        ),
        compiler_params=pltpu.CompilerParams(vmem_limit_bytes=40 * MIB),
        cost_estimate=pl.CostEstimate(
            flops=2 * fields * p_local * q_local * count * width,
            bytes_accessed=2 * fields * p_local * q_local,
            transcendentals=0,
        ),
    )(index, vertex, b_blocks, a_wide)
    return out.reshape(fields, count * width)


def swap(v, axis, bit):
    return lax.ppermute(v, axis, [(s, s ^ bit) for s in range(lax.axis_size(axis))])


def ordered(bit_set, mine, theirs, axis):
    return jnp.where(
        bit_set, jnp.concatenate([theirs, mine], axis), jnp.concatenate([mine, theirs], axis)
    )


def fast(vertex, a_factor, b_factor):
    row, col = lax.axis_index("row"), lax.axis_index("col")
    fields = vertex.shape[0]
    wide = a_factor.shape[1]
    narrow = b_factor.shape[1]
    rank = 4 * wide
    x_bit, z_low, z_high = row & 1, (row >> 1) & 1, row >> 2
    core, y_bit = col & 1, col >> 1
    zz = row >> 1

    b_pair = ordered(x_bit == 1, b_factor, swap(b_factor, "row", 1), 1)
    a_pair = ordered(y_bit == 1, a_factor, swap(a_factor, "col", 2), 1)
    b_far = swap(b_pair, "row", 4)
    a_other = swap(a_pair, "col", 1)
    own, other = a_pair.reshape(-1, 2, wide), a_other.reshape(-1, 2, wide)
    first = jnp.where(core == 1, other, own)
    second = jnp.where(core == 1, own, other)
    a_rows = jnp.stack([first, second], axis=2).reshape(-1, rank)
    a_wide = a_rows.astype(jnp.float32)
    b_half = jnp.stack([b_pair, b_far])
    b_rest = swap(b_half, "row", 2)

    ga = dot_tn(a_rows, a_factor).reshape(4, 2, narrow, wide)
    ga_send = jnp.where(x_bit == 1, ga[:, 0], ga[:, 1])
    ga_keep = jnp.where(x_bit == 1, ga[:, 1], ga[:, 0])
    ga = (ga_keep + swap(ga_send, "row", 1)).reshape(2, 2, narrow, wide)
    ga_send = jnp.where(z_low == 1, ga[:, 0], ga[:, 1])
    ga_keep = jnp.where(z_low == 1, ga[:, 1], ga[:, 0])
    ga = ga_keep + swap(ga_send, "row", 2)
    ga_send = jnp.where(z_high == 1, ga[0], ga[1])
    ga_keep = jnp.where(z_high == 1, ga[1], ga[0])
    ga_tile = ga_keep + swap(ga_send, "row", 4)

    m_pair = contract(zz[None], vertex, b_pair[None], a_wide)
    m_far = contract((zz ^ 2)[None], vertex, b_far[None], a_wide)

    gb_near = jnp.stack([dot_tn(b_pair, b_factor), dot_tn(b_far, b_factor)])
    gb_rest = jnp.stack([dot_tn(b_rest[0], b_factor), dot_tn(b_rest[1], b_factor)])
    odd = (core ^ (zz & 1)) == 1
    gb = jnp.where(odd, gb_rest, gb_near) + swap(jnp.where(odd, gb_near, gb_rest), "col", 1)
    odd = (y_bit ^ (zz >> 1)) == 1
    gb_tile = jnp.where(odd, gb[1], gb[0]) + swap(jnp.where(odd, gb[0], gb[1]), "col", 2)

    down = lax.broadcasted_iota(jnp.int32, (wide, narrow), 0) + col * wide
    across = lax.broadcasted_iota(jnp.int32, (wide, narrow), 1) + row * narrow
    tile = ga_tile.T * gb_tile + jnp.where(down == across, ridge_term, 0.0)

    pieces, tiles = [tile[None]], [[(0, 0)]]
    for axis, bit in (("row", 4), ("row", 2), ("row", 1), ("col", 2)):
        pieces.append(swap(jnp.concatenate(pieces) if len(pieces) > 1 else pieces[0], axis, bit))
        offset = (bit, 0) if axis == "row" else (0, bit)
        tiles.append([(r ^ offset[0], c ^ offset[1]) for piece in tiles for r, c in piece])
    pieces += [swap(piece, "col", 1) for piece in pieces]
    tiles += [[(r, c ^ 1) for r, c in piece] for piece in tiles]

    m_rest = contract(jnp.stack([zz ^ 1, zz ^ 3]), vertex, b_rest, a_wide)
    m_near = ordered(zz >= 2, m_pair, m_far, 0).reshape(2, fields, wide)
    m_rest = m_rest.reshape(fields, 2, wide).transpose(1, 0, 2)
    m_rest = jnp.where(zz >= 2, m_rest[::-1], m_rest)
    m_part = jnp.where(
        z_low == 1, jnp.stack([m_rest, m_near], axis=1), jnp.stack([m_near, m_rest], axis=1)
    )
    m_part = m_part.transpose(2, 0, 1, 3).reshape(2, fields // 2, rank)
    m_half = jnp.where(core == 1, m_part[1], m_part[0])
    m_half = m_half + swap(jnp.where(core == 1, m_part[0], m_part[1]), "col", 1)
    for axis, bit in (("col", 2), ("row", 1), ("row", 2), ("row", 4)):
        m_half = m_half + swap(m_half, axis, bit)
    m_total = ordered(core == 1, m_half, swap(m_half, "col", 1), 0)

    solved = solve(jnp.stack([row, col]), pieces, tiles, m_total)
    return lax.dynamic_slice_in_dim(solved, col * wide, wide, 1)


def general(vertex, a_factor, b_factor):
    fields, p_local, q_local = vertex.shape
    rank_cols, row_rank = a_factor.shape[1], b_factor.shape[1]
    a_rows = lax.all_gather(a_factor, "col", axis=1, tiled=True)
    b_rows = lax.all_gather(b_factor, "row", axis=1, tiled=True)
    rank = a_rows.shape[1]
    a_wide = a_rows.astype(jnp.float32)

    def one_field(slab):
        product = jnp.dot(slab, b_rows, preferred_element_type=jnp.float32)
        return jnp.sum(product * a_wide, axis=0)

    m_total = lax.psum(lax.map(one_field, vertex), ("row", "col"))
    ga_tile = lax.psum_scatter(dot_tn(a_factor, a_rows), "row", scatter_dimension=1, tiled=True)
    gb_tile = lax.psum_scatter(dot_tn(b_factor, b_rows), "col", scatter_dimension=1, tiled=True)
    tiles = lax.all_gather((ga_tile * gb_tile.T)[None], ("row", "col"), axis=0, tiled=True)
    weight = (
        tiles.reshape(lax.axis_size("row"), lax.axis_size("col"), rank_cols, row_rank)
        .transpose(1, 2, 0, 3)
        .reshape(rank, rank)
    )
    weight = weight + ridge_term * jnp.eye(rank, dtype=jnp.float32)
    columns = weight.reshape(rank, rank // NB, NB).transpose(1, 0, 2)
    pieces, tiles = [columns[k][None] for k in range(rank // NB)], [[(k, 0)] for k in range(rank // NB)]
    solved = solve(jnp.zeros((2,), jnp.int32), pieces, tiles, m_total)
    return lax.dynamic_slice_in_dim(solved, lax.axis_index("col") * rank_cols, rank_cols, 1)


def on_device(vertex, a_factor, b_factor):
    rows, cols = lax.axis_size("row"), lax.axis_size("col")
    aligned = a_factor.shape[1] == 2 * NB and b_factor.shape[1] == NB
    if rows == 8 and cols == 4 and aligned:
        return fast(vertex, a_factor, b_factor)
    return general(vertex, a_factor, b_factor)


def solution(mesh):
    return jax.shard_map(
        on_device,
        mesh=mesh,
        in_specs=(P(None, "row", "col"), P("row", "col"), P("col", "row")),
        out_specs=P(None, "col"),
        check_vma=False,
    )
```

```python
import functools

import jax
import jax.numpy as jnp
from jax import lax
from jax.experimental import pallas as pl
from jax.experimental.pallas import tpu as pltpu
from jax.sharding import PartitionSpec as P

ridge_term = 0.25
NB = 128
HIGHEST = lax.Precision.HIGHEST
MIB = 1 << 20


def dot_nt(x, y):
    return lax.dot_general(
        x, y, (((1,), (1,)), ((), ())), precision=HIGHEST, preferred_element_type=jnp.float32
    )


def dot_nn(x, y):
    return lax.dot_general(
        x, y, (((1,), (0,)), ((), ())), precision=HIGHEST, preferred_element_type=jnp.float32
    )


def dot_tn(x, y):
    return lax.dot_general(x, y, (((0,), (0,)), ((), ())), preferred_element_type=jnp.float32)


def row_of(v, j):
    return jnp.broadcast_to(v[j : j + 1, :], v.shape)


def col_of(v, j):
    return jnp.broadcast_to(v[:, j : j + 1], v.shape)


def invert_factor(rows, beside=None):
    count = len(rows)
    lane = lax.broadcasted_iota(jnp.int32, (8, NB), 1)
    sub = lax.broadcasted_iota(jnp.int32, (8, NB), 0)
    rows = list(rows)
    scale = [None] * count
    for g in range(count):
        base = 8 * g
        cur = rows[g]
        cols = [col_of(cur, base + j) for j in range(8)]
        below = [[col_of(rows[i], base + j) for j in range(8)] for i in range(g + 1, count)]
        own = (lane >= base) & (lane < base + 8)
        cur = jnp.where(own, jnp.where(lane == sub + base, 1.0, 0.0), cur)
        forward = cur
        inverse = None
        for j in range(8):
            inv = 1.0 / row_of(cols[j], j)
            here = sub == j
            pivot = row_of(cur, j)
            forward = jnp.where(here, cur, forward)
            inverse = inv if inverse is None else jnp.where(here, inv, inverse)
            mult = cols[j] * inv
            for k in range(j + 1, 8):
                ck = row_of(cols[k], j)
                cols[k] = jnp.where(here, ck * inv, cols[k] - mult * ck)
            cur = jnp.where(here, pivot * inv, cur - mult * pivot)
        picks = [row_of(cur, j) for j in range(8)]
        for t, i in enumerate(range(g + 1, count)):
            prods = [below[t][j] * picks[j] for j in range(8)]
            while len(prods) > 1:
                prods = [prods[s] + prods[s + 1] for s in range(0, len(prods), 2)]
            rows[i] = jnp.where(own, 0.0, rows[i]) - prods[0]
        rows[g] = forward
        scale[g] = jnp.sqrt(inverse)
        if beside is not None:
            beside(g)
    return [jnp.where(lane <= sub + 8 * g, rows[g], 0.0) * scale[g] for g in range(count)]


def span(i, j=None):
    return slice(i * NB, (i + 1 if j is None else j) * NB)


def forward_step(z, k, inverse, work):
    zk = dot_nt(z[:, span(k)], inverse)
    z[:, span(k)] = zk
    nk = work.shape[0]
    if k + 1 < nk:
        z[:, span(k + 1, nk)] -= dot_nt(zk, work[k, span(k + 1, nk), :])


def factor_step(k, work, linv, extra=()):
    nk = work.shape[0]
    jobs = list(extra)

    def tile(i, j):
        work[j, span(i), :] -= dot_nt(work[k - 1, span(i), :], work[k - 1, span(j), :])

    if k:
        jobs += [functools.partial(tile, i, j) for j in range(k + 1, nk) for i in range(j, nk)]
    groups = NB // 8
    rows = [work[k, k * NB + 8 * g : k * NB + 8 * g + 8, :] for g in range(groups)]

    def beside(g):
        for job in jobs[len(jobs) * g // groups : len(jobs) * (g + 1) // groups]:
            job()

    for g, v in enumerate(invert_factor(rows, beside)):
        linv[8 * g : 8 * g + 8, :] = v
    if k + 1 < nk:
        low = span(k + 1, nk)
        panel = dot_nt(work[k, low, :], linv[...])
        work[k, low, :] = panel
        work[k + 1, low, :] -= dot_nt(panel, panel[:NB])


def first_kernel(tiles, pos, *refs):
    pieces, (work, linv, sem) = refs[: len(tiles)], refs[len(tiles) :]
    copies = []
    for piece, offsets in zip(pieces, tiles):
        for t, (row_off, col_off) in enumerate(offsets):
            height = piece.shape[1]
            at = pl.multiple_of((pos[1] ^ col_off) * height, height)
            target = work.at[pos[0] ^ row_off, pl.ds(at, height), :]
            copies.append(pltpu.make_async_copy(piece.at[t], target, sem.at[len(copies)]))
            copies[-1].start()
    for copy in copies:
        copy.wait()
    factor_step(0, work, linv)


def middle_kernel(k, _, work, linv):
    factor_step(k, work, linv)


def near_last_kernel(k, *refs):
    inverses, (mine, theirs, _, work, linv, z) = refs[:k], refs[k:]
    half = mine.shape[0]
    z[:half] = mine[...]
    z[half:] = theirs[...]

    def forward(i):
        forward_step(z, i, inverses[i][...], work)

    factor_step(k, work, linv, [functools.partial(forward, i) for i in range(k)])


def last_kernel(k, before, _, __, work, linv, z):
    def forward():
        forward_step(z, k - 1, before[...], work)

    factor_step(k, work, linv, [forward])


def back_kernel(pos, work, z_ref, *refs):
    nk = work.shape[0]
    inverses, (x_ref, z) = refs[:nk], refs[nk:]
    z[...] = z_ref[...]
    forward_step(z, nk - 1, inverses[nk - 1][...], work)
    for k in reversed(range(nk)):
        xk = dot_nn(z[:, span(k)], inverses[k][...])
        z[:, span(k)] = xk
        for i in reversed(range(k)):
            z[:, span(i)] -= dot_nn(xk, work[i, span(k), :])
    wide = x_ref.shape[1]
    half = x_ref.shape[0] // 2
    mine = pl.ds(pl.multiple_of(pos[1] * wide, wide), wide) if wide % NB == 0 else slice(0, wide)
    start = (pos[1] & 1) * half
    x_ref[pl.ds(pl.multiple_of(start, half), half), :] = z[:half, mine]
    x_ref[pl.ds(pl.multiple_of(half - start, half), half), :] = z[half:, mine]


def in_vmem(body, outs, *args, alias=None, scratch=(), smem=0, flops=10**9, anywhere=0):
    vmem = pl.BlockSpec(memory_space=pltpu.VMEM)
    specs = [pl.BlockSpec(memory_space=pltpu.SMEM)] * smem + [pl.BlockSpec(memory_space=pl.ANY)] * anywhere
    return pl.pallas_call(
        body,
        out_shape=[jax.ShapeDtypeStruct(shape, jnp.dtype(kind)) for shape, kind in outs],
        in_specs=specs + [vmem] * (len(args) - len(specs)),
        out_specs=[vmem] * len(outs),
        scratch_shapes=scratch,
        input_output_aliases=alias or {},
        compiler_params=pltpu.CompilerParams(vmem_limit_bytes=24 * MIB),
        cost_estimate=pl.CostEstimate(flops=flops, bytes_accessed=MIB, transcendentals=0),
    )(*args)


FLOAT = "float32"


def solve(pos, pieces, tiles, rank, hops, m_half, wide, whole_rows):
    nk = rank // NB
    shapes = [((nk, rank, NB), FLOAT), ((NB, NB), FLOAT)]
    count = sum(len(t) for t in tiles)
    steps = [lambda work: in_vmem(functools.partial(first_kernel, tiles), shapes, pos, *pieces,
                                  smem=1, anywhere=len(pieces), scratch=[pltpu.SemaphoreType.DMA((count,))])]
    for k in range(1, nk - 2):
        steps.append(lambda work, k=k: in_vmem(functools.partial(middle_kernel, k), shapes, work, alias={0: 0}))
    work, inverses, hops, theirs = None, [], list(hops), None
    for step in steps:
        if hops:
            coming = hops.pop(0)(m_half)
            work, linv = step(work)
            coming, work = together((coming, work))
            if hops:
                m_half = m_half + coming
                work, m_half = together((work, m_half))
            else:
                theirs = coming
        else:
            work, linv = step(work)
        inverses.append(linv)
    z_shape = ((whole_rows, rank), FLOAT)
    k = nk - 2
    work, linv, z = in_vmem(
        functools.partial(near_last_kernel, k), shapes + [z_shape], *inverses, m_half, theirs, work, alias={k + 2: 0}
    )
    inverses.append(linv)
    work, last, z = in_vmem(
        functools.partial(last_kernel, k + 1), shapes + [z_shape], linv, work, z, alias={1: 0, 2: 2}
    )
    inverses.append(last)
    return in_vmem(
        back_kernel, [((whole_rows, wide), FLOAT)], pos, work, z, *inverses,
        smem=1, scratch=[pltpu.VMEM((whole_rows, rank), jnp.float32)],
    )[0]


def contract_kernel(v_ref, b_ref, a_ref, o_ref, *, base):
    for n in range(b_ref.shape[0]):
        for f in range(v_ref.shape[0]):
            product = jnp.dot(v_ref[f], b_ref[n], preferred_element_type=jnp.float32)
            total = jnp.sum(product * a_ref[base + n], axis=0, keepdims=True)
            o_ref[0, f : f + 1, n * 2 * NB : (n + 1) * 2 * NB] = total


def contract(vertex, start, stop, b_pairs, a_pairs, base):
    _, p_local, q_local = vertex.shape
    width = b_pairs.shape[0] * 2 * NB
    step = 4
    first = start // step
    fields = stop - start
    vmem = pl.BlockSpec(memory_space=pltpu.VMEM)
    out = pl.pallas_call(
        functools.partial(contract_kernel, base=base),
        out_shape=jax.ShapeDtypeStruct((fields // step, step, width), jnp.float32),
        grid=(fields // step,),
        in_specs=[pl.BlockSpec((step, p_local, q_local), lambda i: (i + first, 0, 0)), vmem, vmem],
        out_specs=pl.BlockSpec((1, step, width), lambda i: (i, 0, 0)),
        compiler_params=pltpu.CompilerParams(vmem_limit_bytes=16 * MIB),
        cost_estimate=pl.CostEstimate(
            flops=2 * fields * p_local * q_local * width,
            bytes_accessed=2 * fields * p_local * q_local,
            transcendentals=0,
        ),
    )(vertex, b_pairs, a_pairs)
    return out.reshape(fields, width)


def gram_a_kernel(spots, a_own, a_stack, b_own, b_next, o_ref, a_pairs, b_near):
    for n in range(8):
        block = spots[0] ^ n
        half = pl.multiple_of((block & 1) * NB, NB)
        other = a_stack[(block >> 1) ^ spots[1], :, pl.ds(half, NB)]
        o_ref[n & 1, (n >> 1) & 1, n >> 2] = dot_tn(a_own[...], other)
        a_pairs[n >> 1, :, (n & 1) * NB : (n & 1) * NB + NB] = other.astype(jnp.float32)
    b_near[0, :, :NB] = b_own[...]
    b_near[0, :, NB:] = b_next[...]


def gram_b_kernel(spots, *refs):
    b_refs, (o_ref, b_rest) = refs[:-2], refs[-2:]
    own = b_refs[0][...]
    for off, other in enumerate(b_refs):
        block = spots[0] ^ off
        place = (block >> 1) ^ spots[1]
        half = pl.multiple_of((block & 1) * NB, NB)
        o_ref[place & 1, place >> 1, pl.ds(half, NB), :] = dot_tn(other[...], own)
        if off >= 2:
            b_rest[(off >> 1) - 1, :, (off & 1) * NB : (off & 1) * NB + NB] = other[...]


def place_kernel(parts, spots, *refs):
    m_refs, o_ref = refs[:-1], refs[-1]
    half = o_ref.shape[1]
    for m_ref, (start, offsets) in zip(m_refs, parts):
        stop = start + m_ref.shape[0]
        for lower, upper in ((start, min(stop, half)), (max(start, half), stop)):
            for n, off in enumerate(offsets if lower < upper else ()):
                at = pl.multiple_of((spots[0] ^ off) * NB, NB)
                side = (spots[1] & 1) ^ (lower // half)
                into = slice(lower % half, lower % half + upper - lower)
                o_ref[side, into, pl.ds(at, NB)] = m_ref[lower - start : upper - start, n * NB : (n + 1) * NB]


def swap(v, axis, bit):
    return lax.ppermute(v, axis, [(s, s ^ bit) for s in range(lax.axis_size(axis))])


together = lax.optimization_barrier


def fast(vertex, a_factor, b_factor):
    row, col = lax.axis_index("row"), lax.axis_index("col")
    fields, p_local, q_local = vertex.shape
    wide, narrow = a_factor.shape[1], b_factor.shape[1]
    rank = 4 * wide
    spots = jnp.stack([row, col])
    x, z_low, z_high, y, core = ("row", 1), ("row", 2), ("row", 4), ("col", 2), ("col", 1)
    parts, results = [], []
    near, rest = tuple(range(2)), tuple(range(2, 8))
    pairs = {}

    def piece(start, stop, blocks, gate):
        here, gate = together((pairs[blocks], gate))
        results.append(contract(vertex, start, stop, here, pairs["a"], blocks[0] // 2))
        parts.append((start, blocks))
        return gate

    def after(values):
        values, results[-1] = together((values, results[-1]))
        return values

    b = {0: b_factor}
    b[1], a_y = swap(b_factor, *x), swap(a_factor, *y)
    b[4], b[2] = swap(b_factor, *z_high), swap(b_factor, *z_low)
    a_stack = jnp.stack([a_factor, swap(a_factor, *core), a_y, swap(a_y, *core)])
    ga, pairs["a"], pairs[near] = in_vmem(
        gram_a_kernel,
        [((2, 2, 2, wide, narrow), FLOAT), ((4, p_local, wide), FLOAT), ((1, q_local, wide), "bfloat16")],
        spots, a_factor, a_stack, b_factor, b[1], smem=1,
    )
    ga1 = piece(0, 16, near, ga[1])
    ga_in = swap(ga1, *x)
    b[4], b[2] = after((b[4], b[2]))
    b4, b2 = piece(16, 40, near, (b[4], b[2]))
    b[6], b[5], b[3] = swap(b4, *z_low), swap(b4, *x), swap(b2, *x)
    b[6], b[5], b[3], ga_in = after((b[6], b[5], b[3], ga_in))
    ga = ga[0] + ga_in
    b6, ga1 = piece(40, 64, near, (b[6], ga[1]))
    b[7], ga_in = swap(b6, *x), swap(ga1, *z_low)
    b[7], ga_in = after((b[7], ga_in))
    ga = ga[0] + ga_in
    gb, pairs[rest] = in_vmem(
        gram_b_kernel,
        [((2, 2, wide, narrow), FLOAT), ((3, q_local, wide), "bfloat16")],
        spots, *[b[o] for o in range(8)], smem=1,
    )
    gb = gb[0] + swap(gb[1], *core)
    ga1, gb1 = piece(0, 8, rest, (ga[1], gb[1]))
    ga_in, gb_in = after((swap(ga1, *z_high), swap(gb1, *y)))
    down = lax.broadcasted_iota(jnp.int32, (wide, narrow), 0) + col * wide
    across = lax.broadcasted_iota(jnp.int32, (wide, narrow), 1) + row * narrow
    tile = (ga[0] + ga_in) * (gb[0] + gb_in) + jnp.where(down == across, ridge_term, 0.0)

    s0 = piece(8, 16, rest, tile[None])
    s1 = after(swap(s0, *z_high))
    s01 = piece(16, 24, rest, jnp.concatenate([s0, s1]))
    s2 = after(swap(s01, *z_low))
    s2, s01 = piece(24, 36, rest, (s2, s01))
    s3, s4 = after((swap(s01, *x), swap(s2, *y)))
    s013, s24 = piece(36, 52, rest, (jnp.concatenate([s01, s3]), jnp.concatenate([s2, s4])))
    c013, c24 = swap(s013, *core), swap(s24, *core)
    s5, s6, c013, c24 = after((swap(s013, *y), swap(s24, *x), c013, c24))
    s5, s6 = piece(52, 64, rest, (s5, s6))
    c5, c6 = after((swap(s5, *core), swap(s6, *core)))
    t0, t1 = [(0, 0)], [(4, 0)]

    def moved(ts, axis, bit):
        return [(r ^ bit, c) if axis == "row" else (r, c ^ bit) for r, c in ts]

    t01 = t0 + t1
    t2 = moved(t01, *z_low)
    t013 = t01 + moved(t01, *x)
    t24 = t2 + moved(t2, *y)
    pieces = [s013, s24, s5, s6, c013, c24, c5, c6]
    tiles = [t013, t24, moved(t013, *y), moved(t24, *x)]
    tiles += [moved(t, *core) for t in tiles]

    (m,) = in_vmem(
        functools.partial(place_kernel, parts), [((2, fields // 2, rank), FLOAT)], spots, *results, smem=1
    )
    m_half = m[0] + swap(m[1], *core)
    hops = [functools.partial(swap, axis=axis, bit=bit) for axis, bit in (y, x, z_low, z_high, core)]
    return solve(spots, pieces, tiles, rank, hops, m_half, wide, fields)


def general(vertex, a_factor, b_factor):
    fields, p_local, q_local = vertex.shape
    rank_cols, row_rank = a_factor.shape[1], b_factor.shape[1]
    a_rows = lax.all_gather(a_factor, "col", axis=1, tiled=True)
    b_rows = lax.all_gather(b_factor, "row", axis=1, tiled=True)
    rank = a_rows.shape[1]
    a_wide = a_rows.astype(jnp.float32)

    def one_field(slab):
        product = jnp.dot(slab, b_rows, preferred_element_type=jnp.float32)
        return jnp.sum(product * a_wide, axis=0)

    m_total = lax.psum(lax.map(one_field, vertex), ("row", "col"))
    ga_tile = lax.psum_scatter(dot_tn(a_factor, a_rows), "row", scatter_dimension=1, tiled=True)
    gb_tile = lax.psum_scatter(dot_tn(b_factor, b_rows), "col", scatter_dimension=1, tiled=True)
    tiles = lax.all_gather((ga_tile * gb_tile.T)[None], ("row", "col"), axis=0, tiled=True)
    weight = (
        tiles.reshape(lax.axis_size("row"), lax.axis_size("col"), rank_cols, row_rank)
        .transpose(1, 2, 0, 3)
        .reshape(rank, rank)
    )
    weight = weight + ridge_term * jnp.eye(rank, dtype=jnp.float32)
    columns = weight.reshape(rank, rank // NB, NB).transpose(1, 0, 2)
    pieces, tiles = [columns[k][None] for k in range(rank // NB)], [[(k, 0)] for k in range(rank // NB)]
    half = fields // 2
    hops = [lambda m: m_total[half:]]
    columns = lax.axis_index("col") * rank_cols
    solved = solve(jnp.zeros((2,), jnp.int32), pieces, tiles, rank, hops, m_total[:half], rank, fields)
    return lax.dynamic_slice_in_dim(solved, columns, rank_cols, 1)


def on_device(vertex, a_factor, b_factor):
    rows, cols = lax.axis_size("row"), lax.axis_size("col")
    aligned = a_factor.shape[1] == 2 * NB and b_factor.shape[1] == NB
    if rows == 8 and cols == 4 and aligned:
        return fast(vertex, a_factor, b_factor)
    return general(vertex, a_factor, b_factor)


def solution(mesh):
    return jax.shard_map(
        on_device,
        mesh=mesh,
        in_specs=(P(None, "row", "col"), P("row", "col"), P("col", "row")),
        out_specs=P(None, "col"),
        check_vma=False,
    )
```

```python
import functools

import jax
import jax.numpy as jnp
from jax import lax
from jax.experimental import pallas as pl
from jax.experimental.pallas import tpu as pltpu
from jax.sharding import PartitionSpec as P

ridge_term = 0.25
NB = 128
HIGHEST = lax.Precision.HIGHEST
MIB = 1 << 20


def dot_nt(x, y):
    return lax.dot_general(
        x, y, (((1,), (1,)), ((), ())), precision=HIGHEST, preferred_element_type=jnp.float32
    )


def dot_nn(x, y):
    return lax.dot_general(
        x, y, (((1,), (0,)), ((), ())), precision=HIGHEST, preferred_element_type=jnp.float32
    )


def dot_tn(x, y):
    return lax.dot_general(x, y, (((0,), (0,)), ((), ())), preferred_element_type=jnp.float32)


def row_of(v, j):
    return jnp.broadcast_to(v[j : j + 1, :], v.shape)


def col_of(v, j):
    return jnp.broadcast_to(v[:, j : j + 1], v.shape)


def total(values):
    while len(values) > 1:
        values = [values[s] + values[s + 1] for s in range(0, len(values), 2)]
    return values[0]


def invert_factor(rows, beside=None):
    count = len(rows)
    lane = lax.broadcasted_iota(jnp.int32, (8, NB), 1)
    sub = lax.broadcasted_iota(jnp.int32, (8, NB), 0)
    rows = list(rows)
    scale = [None] * count
    cols = [col_of(rows[0], j) for j in range(8)]
    for g in range(count):
        base = 8 * g
        cur = rows[g]
        below = [[col_of(rows[i], base + j) for j in range(8)] for i in range(g + 1, count)]
        ahead = []
        if g + 1 < count:
            cols = cols + [col_of(cur, base + 8 + j) for j in range(8)]
            ahead = [col_of(rows[g + 1], base + 8 + j) for j in range(8)]
        own = (lane >= base) & (lane < base + 8)
        cur = jnp.where(own, jnp.where(lane == sub + base, 1.0, 0.0), cur)
        forward = cur
        inverse = None
        for j in range(8):
            inv = 1.0 / row_of(cols[j], j)
            here = sub == j
            forward = jnp.where(here, cur, forward)
            inverse = inv if inverse is None else jnp.where(here, inv, inverse)
            mult = jnp.where(here, 0.0, cols[j]) * inv
            for k in range(j + 1, len(cols)):
                cols[k] = cols[k] - mult * row_of(cols[k], j)
            cur = cur - mult * row_of(cur, j)
        cur = cur * inverse
        coming = [c * inverse for c in cols[8:]]
        cols = [a - total([below[0][j] * row_of(c, j) for j in range(8)]) for a, c in zip(ahead, coming)]
        picks = [row_of(cur, j) for j in range(8)]
        for t, i in enumerate(range(g + 1, count)):
            rows[i] = jnp.where(own, 0.0, rows[i]) - total([below[t][j] * picks[j] for j in range(8)])
        rows[g] = forward
        scale[g] = jnp.sqrt(inverse)
        if beside is not None:
            beside(g)
    return [jnp.where(lane <= sub + 8 * g, rows[g], 0.0) * scale[g] for g in range(count)]


def span(i, j=None):
    return slice(i * NB, (i + 1 if j is None else j) * NB)


def forward_step(z, k, inverse, work):
    zk = dot_nt(z[:, span(k)], inverse)
    z[:, span(k)] = zk
    nk = work.shape[0]
    if k + 1 < nk:
        z[:, span(k + 1, nk)] -= dot_nt(zk, work[k, span(k + 1, nk), :])


def factor_step(k, work, linv, before=None, extra=(), arrive=None):
    nk = work.shape[0]
    jobs = []

    def panel(i, j):
        work[k - 1, span(i, j), :] = dot_nt(work[k - 1, span(i, j), :], before[...])

    def update(column, i, j):
        work[column, span(i, j), :] -= dot_nt(work[k - 1, span(i, j), :], work[k - 1, span(column), :])

    def chunks(first):
        return [(i, min(i + 2, nk)) for i in range(first, nk, 2)]

    if k:
        jobs += [functools.partial(panel, i, j) for i, j in chunks(k + 1)]
        for column in range(k, nk):
            jobs += [functools.partial(update, column, i, j) for i, j in chunks(max(column, k + 1))]
    jobs += list(extra)
    groups = NB // 8
    rows = [work[k, k * NB + 8 * g : k * NB + 8 * g + 8, :] for g in range(groups)]

    def beside(g):
        for job in jobs[len(jobs) * g // groups : len(jobs) * (g + 1) // groups]:
            job()

    for g, v in enumerate(invert_factor(rows, beside)):
        linv[8 * g : 8 * g + 8, :] = v
    if arrive is not None:
        arrive()
    if k + 1 < nk:
        panel_next = dot_nt(work[k, span(k + 1), :], linv[...])
        work[k, span(k + 1), :] = panel_next
        work[k + 1, span(k + 1), :] -= dot_nt(panel_next, panel_next)


def first_kernel(tiles, pos, *refs):
    pieces, (work, linv, sem) = refs[: len(tiles)], refs[len(tiles) :]
    nk = work.shape[0]
    for piece, offsets in zip(pieces, tiles):
        for t, (row_off, col_off) in enumerate(offsets):
            height = piece.shape[1]
            column = pos[0] ^ row_off
            at = pl.multiple_of((pos[1] ^ col_off) * height, height)
            pltpu.make_async_copy(piece.at[t], work.at[column, pl.ds(at, height), :], sem.at[column]).start()

    def wait(column):
        pltpu.make_async_copy(work.at[column], work.at[column], sem.at[column]).wait()

    wait(0)

    def arrive():
        for column in range(1, nk):
            wait(column)

    factor_step(0, work, linv, arrive=arrive)


def middle_kernel(k, before, _, work, linv):
    factor_step(k, work, linv, before)


def near_last_kernel(k, *refs):
    inverses, (mine, theirs, _, work, linv, z) = refs[:k], refs[k:]
    half = mine.shape[0]
    z[:half] = mine[...]
    z[half:] = theirs[...]

    def forward(i):
        forward_step(z, i, inverses[i][...], work)

    factor_step(k, work, linv, inverses[k - 1], [functools.partial(forward, i) for i in range(k)])


def last_kernel(k, before, _, __, work, linv, z):
    def forward():
        forward_step(z, k - 1, before[...], work)

    factor_step(k, work, linv, before, [forward])


def back_kernel(pos, work, z_ref, *refs):
    nk = work.shape[0]
    inverses, (x_ref, z) = refs[:nk], refs[nk:]
    z[...] = z_ref[...]
    forward_step(z, nk - 1, inverses[nk - 1][...], work)
    for k in reversed(range(nk)):
        xk = dot_nn(z[:, span(k)], inverses[k][...])
        z[:, span(k)] = xk
        for i in reversed(range(k)):
            z[:, span(i)] -= dot_nn(xk, work[i, span(k), :])
    wide = x_ref.shape[1]
    half = x_ref.shape[0] // 2
    mine = pl.ds(pl.multiple_of(pos[1] * wide, wide), wide) if wide % NB == 0 else slice(0, wide)
    start = (pos[1] & 1) * half
    x_ref[pl.ds(pl.multiple_of(start, half), half), :] = z[:half, mine]
    x_ref[pl.ds(pl.multiple_of(half - start, half), half), :] = z[half:, mine]


def in_vmem(body, outs, *args, alias=None, scratch=(), smem=0, flops=10**9, anywhere=0, limit=24):
    vmem = pl.BlockSpec(memory_space=pltpu.VMEM)
    specs = [pl.BlockSpec(memory_space=pltpu.SMEM)] * smem + [pl.BlockSpec(memory_space=pl.ANY)] * anywhere
    return pl.pallas_call(
        body,
        out_shape=[jax.ShapeDtypeStruct(shape, jnp.dtype(kind)) for shape, kind in outs],
        in_specs=specs + [vmem] * (len(args) - len(specs)),
        out_specs=[vmem] * len(outs),
        scratch_shapes=scratch,
        input_output_aliases=alias or {},
        compiler_params=pltpu.CompilerParams(vmem_limit_bytes=limit * MIB),
        cost_estimate=pl.CostEstimate(flops=flops, bytes_accessed=MIB, transcendentals=0),
    )(*args)


FLOAT = "float32"


def solve(pos, pieces, tiles, rank, hops, m_half, wide, whole_rows):
    nk = rank // NB
    shapes = [((nk, rank, NB), FLOAT), ((NB, NB), FLOAT)]
    steps = [lambda work, before: in_vmem(functools.partial(first_kernel, tiles), shapes, pos, *pieces,
                                  smem=1, anywhere=len(pieces), scratch=[pltpu.SemaphoreType.DMA((nk,))])]
    for k in range(1, nk - 2):
        steps.append(
            lambda work, before, k=k: in_vmem(functools.partial(middle_kernel, k), shapes, before, work, alias={1: 0})
        )
    work, linv, inverses, hops, theirs = None, None, [], list(hops), None
    for step in steps:
        if hops:
            coming = hops.pop(0)(m_half)
            work, linv = step(work, linv)
            coming, work = together((coming, work))
            if hops:
                m_half = m_half + coming
                work, m_half = together((work, m_half))
            else:
                theirs = coming
        else:
            work, linv = step(work, linv)
        inverses.append(linv)
    z_shape = ((whole_rows, rank), FLOAT)
    k = nk - 2
    work, linv, z = in_vmem(
        functools.partial(near_last_kernel, k), shapes + [z_shape], *inverses, m_half, theirs, work, alias={k + 2: 0}
    )
    inverses.append(linv)
    work, last, z = in_vmem(
        functools.partial(last_kernel, k + 1), shapes + [z_shape], linv, work, z, alias={1: 0, 2: 2}
    )
    inverses.append(last)
    return in_vmem(
        back_kernel, [((whole_rows, wide), FLOAT)], pos, work, z, *inverses,
        smem=1, scratch=[pltpu.VMEM((whole_rows, rank), jnp.float32)],
    )[0]


def contract_kernel(_, v_ref, b_ref, a_ref, o_ref, *, base):
    for n in range(b_ref.shape[0]):
        for f in range(v_ref.shape[0]):
            product = jnp.dot(v_ref[f], b_ref[n], preferred_element_type=jnp.float32)
            summed = jnp.sum(product * a_ref[base + n], axis=0, keepdims=True)
            o_ref[0, f : f + 1, n * 2 * NB : (n + 1) * 2 * NB] = summed


def contract(gate, vertex, start, stop, b_pairs, a_pairs, base):
    _, p_local, q_local = vertex.shape
    width = b_pairs.shape[0] * 2 * NB
    step = 4 if b_pairs.shape[0] == 1 else 2
    first = start // step
    fields = stop - start
    vmem = pl.BlockSpec(memory_space=pltpu.VMEM)
    out = pl.pallas_call(
        functools.partial(contract_kernel, base=base),
        out_shape=jax.ShapeDtypeStruct((fields // step, step, width), jnp.float32),
        grid=(fields // step,),
        in_specs=[
            pl.BlockSpec(memory_space=pltpu.SMEM),
            pl.BlockSpec((step, p_local, q_local), lambda i: (i + first, 0, 0)),
            pl.BlockSpec(b_pairs.shape, lambda i: (0, 0, 0)),
            vmem,
        ],
        out_specs=pl.BlockSpec((1, step, width), lambda i: (i, 0, 0)),
        compiler_params=pltpu.CompilerParams(vmem_limit_bytes=16 * MIB),
        cost_estimate=pl.CostEstimate(
            flops=2 * fields * p_local * q_local * width,
            bytes_accessed=2 * fields * p_local * q_local,
            transcendentals=0,
        ),
    )(gate, vertex, b_pairs, a_pairs)
    return out.reshape(fields, width)


def fetch(sources, targets, sem):
    copies = [pltpu.make_async_copy(x, y, sem.at[n]) for n, (x, y) in enumerate(zip(sources, targets))]
    for copy in copies:
        copy.start()
    for copy in copies:
        copy.wait()


def gram_a_kernel(spots, *refs):
    a_refs, b_refs, (ga_send, ga_far, ga_near, a_pairs, b_near, a_all, b_all, sem) = refs[:4], refs[4:6], refs[6:]
    fetch([*a_refs, *b_refs], [a_all.at[n] for n in range(4)] + [b_all.at[n] for n in range(2)], sem)
    own = a_all[0]
    for n in range(8):
        block = spots[0] ^ n
        half = pl.multiple_of((block & 1) * NB, NB)
        other = a_all[(block >> 1) ^ spots[1], :, pl.ds(half, NB)]
        gram = dot_tn(own, other)
        if n & 2:
            ga_send[n & 1, n >> 2] = gram
        else:
            (ga_far if n & 1 else ga_near)[n >> 2] = gram
        a_pairs[n >> 1, :, (n & 1) * NB : (n & 1) * NB + NB] = other.astype(jnp.float32)
    for n in range(2):
        b_near[0, :, n * NB : n * NB + NB] = b_all[n]


def gram_b_kernel(spots, *refs):
    b_refs, (gb_near, gb_send, b_rest, b_all, gb, sem) = refs[:-6], refs[-6:]
    fetch(b_refs, [b_all.at[n] for n in range(8)], sem)
    own = b_all[0]
    for off in range(8):
        block = spots[0] ^ off
        place = (block >> 1) ^ spots[1]
        half = pl.multiple_of((block & 1) * NB, NB)
        gb[place & 1, place >> 1, pl.ds(half, NB), :] = dot_tn(b_all[off], own)
        if off >= 2:
            b_rest[(off >> 1) - 1, :, (off & 1) * NB : (off & 1) * NB + NB] = b_all[off]
    gb_near[...] = gb[0]
    gb_send[...] = gb[1]


def place_kernel(parts, spots, *refs):
    m_refs, o_ref = refs[:-1], refs[-1]
    half = o_ref.shape[1]
    for m_ref, (start, offsets) in zip(m_refs, parts):
        stop = start + m_ref.shape[0]
        for lower, upper in ((start, min(stop, half)), (max(start, half), stop)):
            for n, off in enumerate(offsets if lower < upper else ()):
                at = pl.multiple_of((spots[0] ^ off) * NB, NB)
                side = (spots[1] & 1) ^ (lower // half)
                into = slice(lower % half, lower % half + upper - lower)
                o_ref[side, into, pl.ds(at, NB)] = m_ref[lower - start : upper - start, n * NB : (n + 1) * NB]


def swap(v, axis, bit):
    return lax.ppermute(v, axis, [(s, s ^ bit) for s in range(lax.axis_size(axis))])


together = lax.optimization_barrier


def fast(vertex, a_factor, b_factor):
    row, col = lax.axis_index("row"), lax.axis_index("col")
    fields, p_local, q_local = vertex.shape
    wide, narrow = a_factor.shape[1], b_factor.shape[1]
    rank = 4 * wide
    spots = jnp.stack([row, col])
    x, z_low, z_high, y, core = ("row", 1), ("row", 2), ("row", 4), ("col", 2), ("col", 1)
    parts, results = [], []
    gate_word = jnp.stack([row, col])
    near, rest = tuple(range(2)), tuple(range(2, 8))
    pairs = {}

    def piece(start, stop, blocks, gate):
        here, gate = together((gate_word, gate))
        results.append(contract(here, vertex, start, stop, pairs[blocks], pairs["a"], blocks[0] // 2))
        parts.append((start, blocks))
        return gate

    def after(values):
        values, results[-1] = together((values, results[-1]))
        return values

    b = {0: b_factor}
    b[1], a_y = swap(b_factor, *x), swap(a_factor, *y)
    b[4], b[2] = swap(b_factor, *z_high), swap(b_factor, *z_low)
    ga_send, ga_far, ga_near, pairs["a"], pairs[near] = in_vmem(
        gram_a_kernel,
        [((2, 2, wide, narrow), FLOAT), ((2, wide, narrow), FLOAT), ((2, wide, narrow), FLOAT)]
        + [((4, p_local, wide), FLOAT), ((1, q_local, wide), "bfloat16")],
        spots, a_factor, swap(a_factor, *core), a_y, swap(a_y, *core), b_factor, b[1], smem=1, anywhere=6, limit=24,
        scratch=[
            pltpu.VMEM((4, p_local, wide), jnp.bfloat16),
            pltpu.VMEM((2, q_local, narrow), jnp.bfloat16),
            pltpu.SemaphoreType.DMA((6,)),
        ],
    )
    ga_send = piece(0, 16, near, ga_send)
    ga_in = swap(ga_send, *z_low)
    b[4], b[2] = after((b[4], b[2]))
    b4, b2 = piece(16, 40, near, (b[4], b[2]))
    b[6], b[5], b[3] = swap(b4, *z_low), swap(b4, *x), swap(b2, *x)
    b[6], b[5], b[3], ga_in = after((b[6], b[5], b[3], ga_in))
    ga_far = ga_far + ga_in[1]
    ga_near = ga_near + ga_in[0]
    b6, ga_far = piece(40, 64, near, (b[6], ga_far))
    b[7], ga_in = swap(b6, *x), swap(ga_far, *x)
    b[7], ga_in = after((b[7], ga_in))
    ga_mine = ga_near[0] + ga_in[0]
    ga_send = ga_near[1] + ga_in[1]
    gb_near, gb_send, pairs[rest] = in_vmem(
        gram_b_kernel,
        [((2, wide, narrow), FLOAT), ((2, wide, narrow), FLOAT), ((3, q_local, wide), "bfloat16")],
        spots, *[b[o] for o in range(8)], smem=1, anywhere=8, limit=24,
        scratch=[
            pltpu.VMEM((8, q_local, narrow), jnp.bfloat16),
            pltpu.VMEM((2, 2, wide, narrow), jnp.float32),
            pltpu.SemaphoreType.DMA((8,)),
        ],
    )
    gb_in = swap(gb_send, *core)
    gb_mine = gb_near[0] + gb_in[0]
    gb_send = gb_near[1] + gb_in[1]
    ga_send, gb_send = piece(0, 8, rest, (ga_send, gb_send))
    ga_in, gb_in = after((swap(ga_send, *z_high), swap(gb_send, *y)))
    down = lax.broadcasted_iota(jnp.int32, (wide, narrow), 0) + col * wide
    across = lax.broadcasted_iota(jnp.int32, (wide, narrow), 1) + row * narrow
    tile = (ga_mine + ga_in) * (gb_mine + gb_in) + jnp.where(down == across, ridge_term, 0.0)

    s0 = piece(8, 16, rest, tile[None])
    s1 = after(swap(s0, *z_high))
    s01 = piece(16, 24, rest, jnp.concatenate([s0, s1]))
    s2 = after(swap(s01, *z_low))
    s2, s01 = piece(24, 36, rest, (s2, s01))
    s3, s4 = after((swap(s01, *x), swap(s2, *y)))
    s013, s24 = piece(36, 52, rest, (jnp.concatenate([s01, s3]), jnp.concatenate([s2, s4])))
    c013, c24 = swap(s013, *core), swap(s24, *core)
    s5, s6, c013, c24 = after((swap(s013, *y), swap(s24, *x), c013, c24))
    s5, s6 = piece(52, 64, rest, (s5, s6))
    c5, c6 = after((swap(s5, *core), swap(s6, *core)))
    t0, t1 = [(0, 0)], [(4, 0)]

    def moved(ts, axis, bit):
        return [(r ^ bit, c) if axis == "row" else (r, c ^ bit) for r, c in ts]

    t01 = t0 + t1
    t2 = moved(t01, *z_low)
    t013 = t01 + moved(t01, *x)
    t24 = t2 + moved(t2, *y)
    pieces = [s013, s24, s5, s6, c013, c24, c5, c6]
    tiles = [t013, t24, moved(t013, *y), moved(t24, *x)]
    tiles += [moved(t, *core) for t in tiles]

    (m,) = in_vmem(
        functools.partial(place_kernel, parts), [((2, fields // 2, rank), FLOAT)], spots, *results, smem=1
    )
    m_half = m[0] + swap(m[1], *core)
    hops = [functools.partial(swap, axis=axis, bit=bit) for axis, bit in (y, x, z_low, z_high, core)]
    return solve(spots, pieces, tiles, rank, hops, m_half, wide, fields)


def general(vertex, a_factor, b_factor):
    fields, p_local, q_local = vertex.shape
    rank_cols, row_rank = a_factor.shape[1], b_factor.shape[1]
    a_rows = lax.all_gather(a_factor, "col", axis=1, tiled=True)
    b_rows = lax.all_gather(b_factor, "row", axis=1, tiled=True)
    rank = a_rows.shape[1]
    a_wide = a_rows.astype(jnp.float32)

    def one_field(slab):
        product = jnp.dot(slab, b_rows, preferred_element_type=jnp.float32)
        return jnp.sum(product * a_wide, axis=0)

    m_total = lax.psum(lax.map(one_field, vertex), ("row", "col"))
    ga_tile = lax.psum_scatter(dot_tn(a_factor, a_rows), "row", scatter_dimension=1, tiled=True)
    gb_tile = lax.psum_scatter(dot_tn(b_factor, b_rows), "col", scatter_dimension=1, tiled=True)
    tiles = lax.all_gather((ga_tile * gb_tile.T)[None], ("row", "col"), axis=0, tiled=True)
    weight = (
        tiles.reshape(lax.axis_size("row"), lax.axis_size("col"), rank_cols, row_rank)
        .transpose(1, 2, 0, 3)
        .reshape(rank, rank)
    )
    weight = weight + ridge_term * jnp.eye(rank, dtype=jnp.float32)
    columns = weight.reshape(rank, rank // NB, NB).transpose(1, 0, 2)
    pieces, tiles = [columns[k][None] for k in range(rank // NB)], [[(k, 0)] for k in range(rank // NB)]
    half = fields // 2
    hops = [lambda m: m_total[half:]]
    columns = lax.axis_index("col") * rank_cols
    solved = solve(jnp.zeros((2,), jnp.int32), pieces, tiles, rank, hops, m_total[:half], rank, fields)
    return lax.dynamic_slice_in_dim(solved, columns, rank_cols, 1)


def on_device(vertex, a_factor, b_factor):
    rows, cols = lax.axis_size("row"), lax.axis_size("col")
    aligned = a_factor.shape[1] == 2 * NB and b_factor.shape[1] == NB
    if rows == 8 and cols == 4 and aligned:
        return fast(vertex, a_factor, b_factor)
    return general(vertex, a_factor, b_factor)


def solution(mesh):
    return jax.shard_map(
        on_device,
        mesh=mesh,
        in_specs=(P(None, "row", "col"), P("row", "col"), P("col", "row")),
        out_specs=P(None, "col"),
        check_vma=False,
    )
```

```python
import functools

import jax
import jax.numpy as jnp
from jax import lax
from jax.experimental import pallas as pl
from jax.experimental.pallas import tpu as pltpu
from jax.sharding import PartitionSpec as P

ridge_term = 0.25
NB = 128
HIGHEST = lax.Precision.HIGHEST
MIB = 1 << 20


def dot_nt(x, y):
    return lax.dot_general(
        x, y, (((1,), (1,)), ((), ())), precision=HIGHEST, preferred_element_type=jnp.float32
    )


def dot_nn(x, y):
    return lax.dot_general(
        x, y, (((1,), (0,)), ((), ())), precision=HIGHEST, preferred_element_type=jnp.float32
    )


def dot_tn(x, y):
    return lax.dot_general(x, y, (((0,), (0,)), ((), ())), preferred_element_type=jnp.float32)


def row_of(v, j):
    return jnp.broadcast_to(v[j : j + 1, :], v.shape)


def col_of(v, j):
    return jnp.broadcast_to(v[:, j : j + 1], v.shape)


def total(values):
    while len(values) > 1:
        values = [values[s] + values[s + 1] for s in range(0, len(values), 2)]
    return values[0]


def invert_factor(rows, beside=None):
    count = len(rows)
    lane = lax.broadcasted_iota(jnp.int32, (8, NB), 1)
    sub = lax.broadcasted_iota(jnp.int32, (8, NB), 0)
    rows = list(rows)
    scale = [None] * count
    cols = [col_of(rows[0], j) for j in range(8)]
    for g in range(count):
        base = 8 * g
        cur = rows[g]
        below = [[col_of(rows[i], base + j) for j in range(8)] for i in range(g + 1, count)]
        ahead = []
        if g + 1 < count:
            cols = cols + [col_of(cur, base + 8 + j) for j in range(8)]
            ahead = [col_of(rows[g + 1], base + 8 + j) for j in range(8)]
        own = (lane >= base) & (lane < base + 8)
        cur = jnp.where(own, jnp.where(lane == sub + base, 1.0, 0.0), cur)
        forward = cur
        inverse = None
        for j in range(8):
            inv = 1.0 / row_of(cols[j], j)
            here = sub == j
            forward = jnp.where(here, cur, forward)
            inverse = inv if inverse is None else jnp.where(here, inv, inverse)
            mult = jnp.where(here, 0.0, cols[j]) * inv
            for k in range(j + 1, len(cols)):
                cols[k] = cols[k] - mult * row_of(cols[k], j)
            cur = cur - mult * row_of(cur, j)
        cur = cur * inverse
        coming = [c * inverse for c in cols[8:]]
        cols = [a - total([below[0][j] * row_of(c, j) for j in range(8)]) for a, c in zip(ahead, coming)]
        picks = [row_of(cur, j) for j in range(8)]
        for t, i in enumerate(range(g + 1, count)):
            rows[i] = jnp.where(own, 0.0, rows[i]) - total([below[t][j] * picks[j] for j in range(8)])
        rows[g] = forward
        scale[g] = jnp.sqrt(inverse)
        if beside is not None:
            beside(g)
    return [jnp.where(lane <= sub + 8 * g, rows[g], 0.0) * scale[g] for g in range(count)]


def span(i, j=None):
    return slice(i * NB, (i + 1 if j is None else j) * NB)


def forward_step(z, k, inverse, work):
    zk = dot_nt(z[:, span(k)], inverse)
    z[:, span(k)] = zk
    nk = work.shape[0]
    if k + 1 < nk:
        z[:, span(k + 1, nk)] -= dot_nt(zk, work[k, span(k + 1, nk), :])


def factor_step(k, work, linv, before=None, extra=(), arrive=None):
    nk = work.shape[0]
    jobs = []

    def panel(i, j):
        work[k - 1, span(i, j), :] = dot_nt(work[k - 1, span(i, j), :], before[...])

    def update(column, i, j):
        work[column, span(i, j), :] -= dot_nt(work[k - 1, span(i, j), :], work[k - 1, span(column), :])

    def chunks(first):
        return [(i, min(i + 2, nk)) for i in range(first, nk, 2)]

    if k:
        jobs += [functools.partial(panel, i, j) for i, j in chunks(k + 1)]
        for column in range(k, nk):
            jobs += [functools.partial(update, column, i, j) for i, j in chunks(max(column, k + 1))]
    jobs += list(extra)
    groups = NB // 8
    rows = [work[k, k * NB + 8 * g : k * NB + 8 * g + 8, :] for g in range(groups)]

    def beside(g):
        for job in jobs[len(jobs) * g // groups : len(jobs) * (g + 1) // groups]:
            job()

    for g, v in enumerate(invert_factor(rows, beside)):
        linv[8 * g : 8 * g + 8, :] = v
    if arrive is not None:
        arrive()
    if k + 1 < nk:
        panel_next = dot_nt(work[k, span(k + 1), :], linv[...])
        work[k, span(k + 1), :] = panel_next
        work[k + 1, span(k + 1), :] -= dot_nt(panel_next, panel_next)


def first_kernel(tiles, pos, *refs):
    pieces, (work, linv, sem) = refs[: len(tiles)], refs[len(tiles) :]
    nk = work.shape[0]
    for piece, offsets in zip(pieces, tiles):
        for t, (row_off, col_off) in enumerate(offsets):
            height = piece.shape[1]
            column = pos[0] ^ row_off
            at = pl.multiple_of((pos[1] ^ col_off) * height, height)
            pltpu.make_async_copy(piece.at[t], work.at[column, pl.ds(at, height), :], sem.at[column]).start()

    def wait(column):
        pltpu.make_async_copy(work.at[column], work.at[column], sem.at[column]).wait()

    wait(0)

    def arrive():
        for column in range(1, nk):
            wait(column)

    factor_step(0, work, linv, arrive=arrive)


def middle_kernel(k, before, _, work, linv):
    factor_step(k, work, linv, before)


def near_last_kernel(k, *refs):
    inverses, (mine, theirs, _, work, linv, z) = refs[:k], refs[k:]
    half = mine.shape[0]
    z[:half] = mine[...]
    z[half:] = theirs[...]

    def forward(i):
        forward_step(z, i, inverses[i][...], work)

    factor_step(k, work, linv, inverses[k - 1], [functools.partial(forward, i) for i in range(k)])


def last_kernel(k, before, _, __, work, linv, z):
    def forward():
        forward_step(z, k - 1, before[...], work)

    factor_step(k, work, linv, before, [forward])


def back_kernel(pos, work, z_ref, *refs):
    nk = work.shape[0]
    inverses, (x_ref, z) = refs[:nk], refs[nk:]
    z[...] = z_ref[...]
    forward_step(z, nk - 1, inverses[nk - 1][...], work)
    for k in reversed(range(nk)):
        xk = dot_nn(z[:, span(k)], inverses[k][...])
        z[:, span(k)] = xk
        for i in reversed(range(k)):
            z[:, span(i)] -= dot_nn(xk, work[i, span(k), :])
    wide = x_ref.shape[1]
    half = x_ref.shape[0] // 2
    mine = pl.ds(pl.multiple_of(pos[1] * wide, wide), wide) if wide % NB == 0 else slice(0, wide)
    start = (pos[1] & 1) * half
    x_ref[pl.ds(pl.multiple_of(start, half), half), :] = z[:half, mine]
    x_ref[pl.ds(pl.multiple_of(half - start, half), half), :] = z[half:, mine]


def in_vmem(body, outs, *args, alias=None, scratch=(), smem=0, flops=10**9, anywhere=0, limit=24):
    vmem = pl.BlockSpec(memory_space=pltpu.VMEM)
    specs = [pl.BlockSpec(memory_space=pltpu.SMEM)] * smem + [pl.BlockSpec(memory_space=pl.ANY)] * anywhere
    return pl.pallas_call(
        body,
        out_shape=[jax.ShapeDtypeStruct(shape, jnp.dtype(kind)) for shape, kind in outs],
        in_specs=specs + [vmem] * (len(args) - len(specs)),
        out_specs=[vmem] * len(outs),
        scratch_shapes=scratch,
        input_output_aliases=alias or {},
        compiler_params=pltpu.CompilerParams(vmem_limit_bytes=limit * MIB),
        cost_estimate=pl.CostEstimate(flops=flops, bytes_accessed=MIB, transcendentals=0),
    )(*args)


FLOAT = "float32"


def solve(pos, pieces, tiles, rank, hops, m_half, wide, whole_rows):
    nk = rank // NB
    shapes = [((nk, rank, NB), FLOAT), ((NB, NB), FLOAT)]
    steps = [lambda work, before: in_vmem(functools.partial(first_kernel, tiles), shapes, pos, *pieces,
                                  smem=1, anywhere=len(pieces), scratch=[pltpu.SemaphoreType.DMA((nk,))])]
    for k in range(1, nk - 2):
        steps.append(
            lambda work, before, k=k: in_vmem(functools.partial(middle_kernel, k), shapes, before, work, alias={1: 0})
        )
    work, linv, inverses, hops, theirs = None, None, [], list(hops), None
    for step in steps:
        if hops:
            coming = hops.pop(0)(m_half)
            work, linv = step(work, linv)
            coming, work = together((coming, work))
            if hops:
                m_half = m_half + coming
                work, m_half = together((work, m_half))
            else:
                theirs = coming
        else:
            work, linv = step(work, linv)
        inverses.append(linv)
    z_shape = ((whole_rows, rank), FLOAT)
    k = nk - 2
    work, linv, z = in_vmem(
        functools.partial(near_last_kernel, k), shapes + [z_shape], *inverses, m_half, theirs, work, alias={k + 2: 0}
    )
    inverses.append(linv)
    work, last, z = in_vmem(
        functools.partial(last_kernel, k + 1), shapes + [z_shape], linv, work, z, alias={1: 0, 2: 2}
    )
    inverses.append(last)
    return in_vmem(
        back_kernel, [((whole_rows, wide), FLOAT)], pos, work, z, *inverses,
        smem=1, scratch=[pltpu.VMEM((whole_rows, rank), jnp.float32)],
    )[0]


def contract_kernel(_, v_ref, b_ref, a_ref, o_ref, *, base):
    for n in range(b_ref.shape[0]):
        for f in range(v_ref.shape[0]):
            product = jnp.dot(v_ref[f], b_ref[n], preferred_element_type=jnp.float32)
            summed = jnp.sum(product * a_ref[base + n], axis=0, keepdims=True)
            o_ref[0, f : f + 1, n * 2 * NB : (n + 1) * 2 * NB] = summed


def contract(gate, vertex, start, stop, b_pairs, a_pairs, base):
    _, p_local, q_local = vertex.shape
    width = b_pairs.shape[0] * 2 * NB
    step = 4 if b_pairs.shape[0] == 1 else 2
    first = start // step
    fields = stop - start
    vmem = pl.BlockSpec(memory_space=pltpu.VMEM)
    out = pl.pallas_call(
        functools.partial(contract_kernel, base=base),
        out_shape=jax.ShapeDtypeStruct((fields // step, step, width), jnp.float32),
        grid=(fields // step,),
        in_specs=[
            pl.BlockSpec(memory_space=pltpu.SMEM),
            pl.BlockSpec((step, p_local, q_local), lambda i: (i + first, 0, 0)),
            pl.BlockSpec(b_pairs.shape, lambda i: (0, 0, 0)),
            vmem,
        ],
        out_specs=pl.BlockSpec((1, step, width), lambda i: (i, 0, 0)),
        compiler_params=pltpu.CompilerParams(vmem_limit_bytes=16 * MIB),
        cost_estimate=pl.CostEstimate(
            flops=2 * fields * p_local * q_local * width,
            bytes_accessed=2 * fields * p_local * q_local,
            transcendentals=0,
        ),
    )(gate, vertex, b_pairs, a_pairs)
    return out.reshape(fields, width)


def fetch(sources, targets, sem):
    copies = [pltpu.make_async_copy(x, y, sem.at[n]) for n, (x, y) in enumerate(zip(sources, targets))]
    for copy in copies:
        copy.start()
    for copy in copies:
        copy.wait()


def gram_a_kernel(spots, *refs):
    a_refs, b_refs, (ga_send, ga_far, ga_near, a_pairs, b_near, a_all, b_all, sem) = refs[:4], refs[4:6], refs[6:]
    fetch([*a_refs, *b_refs], [a_all.at[n] for n in range(4)] + [b_all.at[n] for n in range(2)], sem)
    own = a_all[0]
    for n in range(8):
        block = spots[0] ^ n
        half = pl.multiple_of((block & 1) * NB, NB)
        other = a_all[(block >> 1) ^ spots[1], :, pl.ds(half, NB)]
        gram = dot_tn(own, other)
        if n & 2:
            ga_send[n & 1, n >> 2] = gram
        else:
            (ga_far if n & 1 else ga_near)[n >> 2] = gram
        a_pairs[n >> 1, :, (n & 1) * NB : (n & 1) * NB + NB] = other.astype(jnp.float32)
    for n in range(2):
        b_near[0, :, n * NB : n * NB + NB] = b_all[n]


def gram_b_kernel(spots, *refs):
    b_refs, (gb_near, gb_send, b_rest, b_all, gb, sem) = refs[:-6], refs[-6:]
    fetch(b_refs, [b_all.at[n] for n in range(8)], sem)
    own = b_all[0]
    for off in range(8):
        block = spots[0] ^ off
        place = (block >> 1) ^ spots[1]
        half = pl.multiple_of((block & 1) * NB, NB)
        gb[place & 1, place >> 1, pl.ds(half, NB), :] = dot_tn(b_all[off], own)
        if off >= 2:
            b_rest[(off >> 1) - 1, :, (off & 1) * NB : (off & 1) * NB + NB] = b_all[off]
    gb_near[...] = gb[0]
    gb_send[...] = gb[1]


def place_kernel(parts, spots, *refs):
    m_refs, o_ref = refs[:-1], refs[-1]
    half = o_ref.shape[1]
    for m_ref, (start, offsets) in zip(m_refs, parts):
        stop = start + m_ref.shape[0]
        for lower, upper in ((start, min(stop, half)), (max(start, half), stop)):
            for n, off in enumerate(offsets if lower < upper else ()):
                at = pl.multiple_of((spots[0] ^ off) * NB, NB)
                side = (spots[1] & 1) ^ (lower // half)
                into = slice(lower % half, lower % half + upper - lower)
                o_ref[side, into, pl.ds(at, NB)] = m_ref[lower - start : upper - start, n * NB : (n + 1) * NB]


def swap(v, axis, bit):
    return lax.ppermute(v, axis, [(s, s ^ bit) for s in range(lax.axis_size(axis))])


together = lax.optimization_barrier


def fast(vertex, a_factor, b_factor):
    row, col = lax.axis_index("row"), lax.axis_index("col")
    fields, p_local, q_local = vertex.shape
    wide, narrow = a_factor.shape[1], b_factor.shape[1]
    rank = 4 * wide
    spots = jnp.stack([row, col])
    x, z_low, z_high, y, core = ("row", 1), ("row", 2), ("row", 4), ("col", 2), ("col", 1)
    parts, results = [], []
    gate_word = jnp.stack([row, col])
    near, rest = tuple(range(2)), tuple(range(2, 8))
    pairs = {}

    def piece(start, stop, blocks, gate):
        here, gate = together((gate_word, gate))
        results.append(contract(here, vertex, start, stop, pairs[blocks], pairs["a"], blocks[0] // 2))
        parts.append((start, blocks))
        return gate

    def after(values):
        values, results[-1] = together((values, results[-1]))
        return values

    b = {0: b_factor}
    b[1], a_y = swap(b_factor, *x), swap(a_factor, *y)
    b[4], b[2] = swap(b_factor, *z_high), swap(b_factor, *z_low)
    ga_send, ga_far, ga_near, pairs["a"], pairs[near] = in_vmem(
        gram_a_kernel,
        [((2, 2, wide, narrow), FLOAT), ((2, wide, narrow), FLOAT), ((2, wide, narrow), FLOAT)]
        + [((4, p_local, wide), FLOAT), ((1, q_local, wide), "bfloat16")],
        spots, a_factor, swap(a_factor, *core), a_y, swap(a_y, *core), b_factor, b[1], smem=1, anywhere=6, limit=24,
        scratch=[
            pltpu.VMEM((4, p_local, wide), jnp.bfloat16),
            pltpu.VMEM((2, q_local, narrow), jnp.bfloat16),
            pltpu.SemaphoreType.DMA((6,)),
        ],
    )
    ga_send = piece(0, 16, near, ga_send)
    ga_in = swap(ga_send, *z_low)
    b[4], b[2] = after((b[4], b[2]))
    b4, b2 = piece(16, 40, near, (b[4], b[2]))
    b[6], b[5], b[3] = swap(b4, *z_low), swap(b4, *x), swap(b2, *x)
    b[6], b[5], b[3], ga_in = after((b[6], b[5], b[3], ga_in))
    ga_far = ga_far + ga_in[1]
    ga_near = ga_near + ga_in[0]
    b6, ga_far = piece(40, 64, near, (b[6], ga_far))
    b[7], ga_in = swap(b6, *x), swap(ga_far, *x)
    b[7], ga_in = after((b[7], ga_in))
    ga_mine = ga_near[0] + ga_in[0]
    ga_send = ga_near[1] + ga_in[1]
    gb_near, gb_send, pairs[rest] = in_vmem(
        gram_b_kernel,
        [((2, wide, narrow), FLOAT), ((2, wide, narrow), FLOAT), ((3, q_local, wide), "bfloat16")],
        spots, *[b[o] for o in range(8)], smem=1, anywhere=8, limit=24,
        scratch=[
            pltpu.VMEM((8, q_local, narrow), jnp.bfloat16),
            pltpu.VMEM((2, 2, wide, narrow), jnp.float32),
            pltpu.SemaphoreType.DMA((8,)),
        ],
    )
    gb_in = swap(gb_send, *core)
    gb_mine = gb_near[0] + gb_in[0]
    gb_send = gb_near[1] + gb_in[1]
    ga_send, gb_send = piece(0, 10, rest, (ga_send, gb_send))
    ga_in, gb_in = after((swap(ga_send, *z_high), swap(gb_send, *y)))
    down = lax.broadcasted_iota(jnp.int32, (wide, narrow), 0) + col * wide
    across = lax.broadcasted_iota(jnp.int32, (wide, narrow), 1) + row * narrow
    tile = (ga_mine + ga_in) * (gb_mine + gb_in) + jnp.where(down == across, ridge_term, 0.0)

    s0 = piece(10, 20, rest, tile[None])
    s1 = after(swap(s0, *z_high))
    s01 = piece(20, 30, rest, jnp.concatenate([s0, s1]))
    s2 = after(swap(s01, *z_low))
    s2, s01 = piece(30, 44, rest, (s2, s01))
    s3, s4 = after((swap(s01, *x), swap(s2, *y)))
    s013, s24 = piece(44, 64, rest, (jnp.concatenate([s01, s3]), jnp.concatenate([s2, s4])))
    c013, c24 = swap(s013, *core), swap(s24, *core)
    s5, s6, c013, c24 = after((swap(s013, *y), swap(s24, *x), c013, c24))
    c5, c6 = swap(s5, *core), swap(s6, *core)
    t0, t1 = [(0, 0)], [(4, 0)]

    def moved(ts, axis, bit):
        return [(r ^ bit, c) if axis == "row" else (r, c ^ bit) for r, c in ts]

    t01 = t0 + t1
    t2 = moved(t01, *z_low)
    t013 = t01 + moved(t01, *x)
    t24 = t2 + moved(t2, *y)
    pieces = [s013, s24, s5, s6, c013, c24, c5, c6]
    tiles = [t013, t24, moved(t013, *y), moved(t24, *x)]
    tiles += [moved(t, *core) for t in tiles]

    (m,) = in_vmem(
        functools.partial(place_kernel, parts), [((2, fields // 2, rank), FLOAT)], spots, *results, smem=1
    )
    m_half = m[0] + swap(m[1], *core)
    hops = [functools.partial(swap, axis=axis, bit=bit) for axis, bit in (y, x, z_low, z_high, core)]
    return solve(spots, pieces, tiles, rank, hops, m_half, wide, fields)


def general(vertex, a_factor, b_factor):
    fields, p_local, q_local = vertex.shape
    rank_cols, row_rank = a_factor.shape[1], b_factor.shape[1]
    a_rows = lax.all_gather(a_factor, "col", axis=1, tiled=True)
    b_rows = lax.all_gather(b_factor, "row", axis=1, tiled=True)
    rank = a_rows.shape[1]
    a_wide = a_rows.astype(jnp.float32)

    def one_field(slab):
        product = jnp.dot(slab, b_rows, preferred_element_type=jnp.float32)
        return jnp.sum(product * a_wide, axis=0)

    m_total = lax.psum(lax.map(one_field, vertex), ("row", "col"))
    ga_tile = lax.psum_scatter(dot_tn(a_factor, a_rows), "row", scatter_dimension=1, tiled=True)
    gb_tile = lax.psum_scatter(dot_tn(b_factor, b_rows), "col", scatter_dimension=1, tiled=True)
    tiles = lax.all_gather((ga_tile * gb_tile.T)[None], ("row", "col"), axis=0, tiled=True)
    weight = (
        tiles.reshape(lax.axis_size("row"), lax.axis_size("col"), rank_cols, row_rank)
        .transpose(1, 2, 0, 3)
        .reshape(rank, rank)
    )
    weight = weight + ridge_term * jnp.eye(rank, dtype=jnp.float32)
    columns = weight.reshape(rank, rank // NB, NB).transpose(1, 0, 2)
    pieces, tiles = [columns[k][None] for k in range(rank // NB)], [[(k, 0)] for k in range(rank // NB)]
    half = fields // 2
    hops = [lambda m: m_total[half:]]
    columns = lax.axis_index("col") * rank_cols
    solved = solve(jnp.zeros((2,), jnp.int32), pieces, tiles, rank, hops, m_total[:half], rank, fields)
    return lax.dynamic_slice_in_dim(solved, columns, rank_cols, 1)


def on_device(vertex, a_factor, b_factor):
    rows, cols = lax.axis_size("row"), lax.axis_size("col")
    aligned = a_factor.shape[1] == 2 * NB and b_factor.shape[1] == NB
    if rows == 8 and cols == 4 and aligned:
        return fast(vertex, a_factor, b_factor)
    return general(vertex, a_factor, b_factor)


def solution(mesh):
    return jax.shard_map(
        on_device,
        mesh=mesh,
        in_specs=(P(None, "row", "col"), P("row", "col"), P("col", "row")),
        out_specs=P(None, "col"),
        check_vma=False,
    )
```
